128 devices in a mesh: seq: 32 (over x, y, core), trk: 4 (over z).
Axes of the slice: x: 4, y: 4, z: 4, core: 2. Of those that a mesh axis runs over, the one named last changes fastest.
Arguments:
- trunk_input: bfloat16 [12288, 1536], P('seq', 'trk'), may hold values from -6 to 6
- conv_in: bfloat16 [6, 3, 768, 1536], P(None, None, 'trk'), may hold values from -0.09375 to 0.09375
- conv_bias: bfloat16 [6, 768], P(None, 'trk'), may hold values from -3 to 3
- conv_out: bfloat16 [6, 768, 1536], P(None, 'trk'), may hold values from -0.21875 to 0.21875
- projection_bias: bfloat16 [6, 1536], P(None, 'trk'), may hold values from -3 to 3
- head_weight: bfloat16 [1536, 4096], P(None, 'trk'), may hold values from -0.15625 to 0.15625
- head_bias: bfloat16 [4096], P('trk'), may hold values from -4 to 4
- exon_bins: int32 [256, 64], P('seq'), may hold values from -1 to 12287, as said below
Outputs:
- coverage: bfloat16 [12288, 4096], P('seq', 'trk')
- gene_cov: float32 [256, 4096], P('seq', 'trk')
The draws below stay inside these ranges and needn't reach their ends.
Inputs may be any that keep to these rules, and one draw needn't show every extreme that they name: `exon_bins`: row g lists gene g's exon bins in increasing order, then -1 in the unused entries; every gene has at least one exon bin and some gene has exactly 64. The genes of rows 8 * o to 8 * (o + 1) - 1 are owned by index o of seq.
All inputs are finite; a program needn't handle non-finite values.
Results may differ from the reference program's by a relative error of at most 0.024.
Values may be sent and summed in bfloat16 or wider, within the bound.
A program may use at most 128 MiB of HBM per device.

```python
import jax
import jax.numpy as jnp
from jax import lax

C = 1536
HID = 768
TRACKS = 4096
RESIDUAL_BLOCKS = 6
BASE_DILATION = 2
EXON_MAX = 64
BINS = 12288
GENES = 256
N_TRK = 4


def draw_exon_bins(key, part):
    key_count, key_stride, key_pick, key_other, key_start = jax.random.split(jax.random.fold_in(key, 11), 5)
    counts = jax.random.randint(key_count, (GENES,), 1, EXON_MAX + 1)
    stride = jax.random.randint(key_stride, (GENES,), 1, 9)
    chosen = jax.random.randint(key_pick, (), 0, GENES)
    second = (chosen + 1 + jax.random.randint(key_other, (), 0, GENES - 1)) % GENES
    gene_ids = jnp.arange(GENES)
    counts = jnp.where(gene_ids == chosen, EXON_MAX, jnp.where(gene_ids == second, 1, counts))
    extent = (counts - 1) * stride
    starts = jax.random.randint(key_start, (GENES,), 0, BINS - 8 * EXON_MAX + 1)
    starts = jnp.where(gene_ids == chosen, BINS - 1 - extent, starts)
    entry = jnp.arange(EXON_MAX)
    positions = starts[:, None] + entry[None, :] * stride[:, None]
    return jnp.where(entry[None, :] < counts[:, None], positions, -1).astype(jnp.int32)


def shard_levels(key, shape, shards, least, high):
    def one(dim, blocks):
        heights = jax.random.uniform(jax.random.fold_in(jax.random.fold_in(key, 6), dim), (blocks,), jnp.float32, least / len(shards), high / len(shards))
        return jnp.repeat(jnp.exp(heights), shape[dim] // blocks).reshape((-1,) + (1,) * (len(shape) - dim - 1))

    loudness = one(*shards[0])
    for cut in shards[1:]:
        loudness = loudness * one(*cut)
    return loudness


def bell_draw(key, shape, width, limit, pieces=(), kind=jnp.bfloat16):
    array = jax.random.normal(key, shape, jnp.float32) * width
    if len(pieces) > 0:
        array = shard_levels(key, shape, pieces, -0.22, 0.18) * array
    return jnp.clip(array, min=-limit, max=limit).astype(kind)


def setup_inputs(seed: int = 0) -> dict:
    key_list = jax.random.split(jax.random.key(seed), 9)
    return {
        "trunk_input": bell_draw(key_list[0], (BINS, C), 1.0, 6.0, ((0, 32), (1, 4))),
        "conv_in": bell_draw(key_list[1], (RESIDUAL_BLOCKS, 3, HID, C), (3 * C) ** -0.5, 0.09375, ((2, 4),)),
        "conv_bias": bell_draw(key_list[2], (RESIDUAL_BLOCKS, HID), 0.5, 3.0, ((1, 4),)),
        "conv_out": bell_draw(key_list[3], (RESIDUAL_BLOCKS, HID, C), HID ** -0.5, 0.21875, ((1, 4),)),
        "projection_bias": bell_draw(key_list[4], (RESIDUAL_BLOCKS, C), 0.5, 3.0, ((1, 4),)),
        "head_weight": bell_draw(key_list[5], (C, TRACKS), C ** -0.5, 0.15625, ((1, 4),)),
        "head_bias": bell_draw(key_list[6], (TRACKS,), 1.0, 4.0, ((0, 4),)),
        "exon_bins": draw_exon_bins(jax.random.fold_in(key_list[8], 71), 0),
    }


def contract_last(rows, kernel):
    return lax.dot_general(rows, kernel, (((1,), (1,)), ((), ())), preferred_element_type=jnp.float32)


def reference(trunk_input, conv_in, conv_bias, conv_out, projection_bias, head_weight, head_bias, exon_bins):
    trunk = trunk_input
    group_width = HID // N_TRK
    for block_layer_index in range(RESIDUAL_BLOCKS):
        dilation_step = BASE_DILATION * 2 ** block_layer_index
        padded = jnp.pad(trunk, ((dilation_step, dilation_step), (0, 0)))
        inner = jnp.zeros((BINS, HID), jnp.float32)
        for tap_index in range(3):
            window = padded[tap_index * dilation_step: tap_index * dilation_step + BINS]
            inner = inner + contract_last(window, conv_in[block_layer_index, tap_index])
        activation = jax.nn.gelu(inner + conv_bias[block_layer_index].astype(jnp.float32), approximate=True).astype(jnp.bfloat16)
        branch = jnp.zeros((BINS, C), jnp.float32)
        for group_index in range(N_TRK):
            lower = group_index * group_width
            partial_value = jnp.dot(activation[:, lower:lower + group_width], conv_out[block_layer_index, lower:lower + group_width], preferred_element_type=jnp.float32)
            rounded = lax.optimization_barrier(partial_value.astype(jnp.bfloat16))
            branch = branch + rounded.astype(jnp.float32)
        trunk = (trunk.astype(jnp.float32) + branch + projection_bias[block_layer_index].astype(jnp.float32)).astype(jnp.bfloat16)
    logits = jnp.dot(trunk, head_weight, preferred_element_type=jnp.float32)
    coverage = jax.nn.softplus(logits + head_bias.astype(jnp.float32)).astype(jnp.bfloat16)
    present = exon_bins >= 0
    safe_index = jnp.where(present, exon_bins, 0).astype(jnp.int32)
    picked = coverage[safe_index].astype(jnp.float32)
    gene_sum = jnp.sum(jnp.where(present[:, :, None], picked, jnp.float32(0.0)), axis=1)
    counts = jnp.sum(present.astype(jnp.float32), axis=1)
    gene_cov = gene_sum / counts[:, None]
    return coverage, gene_cov
```

```python
import functools

import jax
import jax.numpy as jnp
from jax import lax
from jax.experimental import pallas as pl
from jax.experimental.pallas import tpu as pltpu
from jax.sharding import PartitionSpec as P

MESH = pl.DeviceIdType.MESH
BLOCKS = 6
BASE_DILATION = 2
RING = 4
ROWS = 384
C = 1536
HID = 192
HALO = 64
TRACKS = 1024
GENES = 256
EXONS = 64
G = 96
GROUPS = ((0, 3), (1, 2))


def remote(src, dst, send, recv, device):
    return pltpu.make_async_remote_copy(
        src_ref=src, dst_ref=dst, send_sem=send, recv_sem=recv, device_id=device, device_id_type=MESH
    )


class Ring:
    def __init__(self, region, me, right, left, send, recv, own=None):
        self.region, self.me, self.right, self.left = region, me, right, left
        self.send, self.recv = send, recv
        self.own = own or (lambda part: region(me, part))
        self.before, self.after = lax.rem(me + RING - 1, RING), lax.rem(me + 1, RING)
        self.across = lax.rem(me + 2, RING)

    def copy(self, src, origin, part, way, device):
        return remote(src, self.region(origin, part), self.send(part * 3 + way), self.recv(part * 3 + way), device)

    def start(self, part):
        ways = ((0, self.right), (1, self.left))
        for way, device in ways:
            self.copy(self.own(part), self.me, part, way, device).start()

    def arrived(self, origin, part, way):
        there = self.region(origin, part)
        remote(there, there, self.send(part * 3 + way), self.recv(part * 3 + way), self.right).wait_recv()

    def relay(self, part):
        origin, device = (self.before, self.right) if part == 0 else (self.after, self.left)
        self.arrived(origin, part, part)
        self.copy(self.region(origin, part), origin, part, 2, device).start()

    def gathered(self, part):
        if part == 0:
            self.arrived(self.after, 0, 1)
        else:
            self.arrived(self.before, 1, 0)
        self.arrived(self.across, part, 2)

    def sent(self):
        for part in (0, 1):
            for way in (0, 1, 2):
                there = self.own(part) if way < 2 else self.region(self.me, part)
                remote(there, self.region(self.me, part), self.send(part * 3 + way), self.recv(part * 3 + way), self.right).wait_send()


def gelu(v):
    return v * (0.5 * (1.0 + jnp.tanh(0.7978845608028654 * (v + 0.044715 * (v * v * v)))))


def softplus(logits):
    return jnp.maximum(logits, 0.0) + jnp.log1p(jnp.exp(-jnp.abs(logits)))


def kernel(
    x_ref, conv_in_ref, conv_bias_ref, conv_out_ref, pbias_ref, head_ref, head_bias_ref, exon_ref,
    cov_out, gene_out,
    trunk, w_in, w_out, w_head, taps, inner, acts, bias_in, bias_out, pbias_all, cov, exon_all, onehot,
    own_sum, gene_a, gene_ar, gene_b, gene_br, gene_c, gene_cr,
    local, trunk_s, trunk_r, act_s, act_r, wz_s, wz_r, wr_s, wr_r, wc_s, wc_r,
    halo_s, halo_r, pb_s, pb_r, ex_s, ex_r, ga_s, ga_r, gb_s, gb_r, gc_s, gc_r,
):
    p = lax.axis_index("seq")
    z = lax.axis_index("trk")
    core = lax.rem(p, 2)
    y = lax.rem(p // 2, RING)
    x = p // 8
    last = 31

    def at(xx, yy, cc):
        return (lax.rem(xx, RING) * RING + lax.rem(yy, RING)) * 2 + cc

    z_right, z_left = (p, lax.rem(z + 1, RING)), (p, lax.rem(z + 3, RING))
    partner = (p + 1 - 2 * core, z)
    ring_me = x * (1 - core) + y * core
    ring_right = (at(x + 1 - core, y + core, core), z)
    ring_left = (at(x + 3 * (1 - core), y + 3 * core, core), z)
    x_peers = [(at(x + d, y, core), z) for d in (1, 2, 3)]
    y_peers = [(at(x, y + d, core), z) for d in (1, 2, 3)]
    z_peers = [(p, lax.rem(z + d, RING)) for d in (1, 2, 3)]

    barrier = pltpu.get_barrier_semaphore()
    for device in [partner] + x_peers + y_peers + z_peers:
        pl.semaphore_signal(barrier, inc=1, device_id=device, device_id_type=MESH)
    far = p + 2 * core - 1
    has_far = jnp.logical_and(far >= 0, far <= last)

    @pl.when(has_far)
    def _():
        pl.semaphore_signal(barrier, inc=1, device_id=(far, z), device_id_type=MESH)

    def load_in(b):
        return pltpu.make_async_copy(conv_in_ref.at[b], w_in.at[b], local.at[b])

    rows_at, cols_at = pl.multiple_of(core * G, 16), pl.multiple_of(ring_me * 384, 128)

    def load_out(b):
        src = conv_out_ref.at[b, pl.ds(rows_at, G), pl.ds(cols_at, 384)]
        return pltpu.make_async_copy(src, w_out.at[b, z, core, :, pl.ds(cols_at, 384)], local.at[BLOCKS + b])

    z_cols = pl.multiple_of(z * 384, 128)
    load_x = pltpu.make_async_copy(x_ref, trunk.at[0, pl.ds(HALO, ROWS), pl.ds(z_cols, 384)], local.at[12])
    load_head = pltpu.make_async_copy(head_ref, w_head, local.at[13])
    gene_at = pl.multiple_of(core * 128 + x * 32 + y * 8, 8)
    load_exon = pltpu.make_async_copy(exon_ref, exon_all.at[pl.ds(gene_at, 8)], local.at[14])
    load_x.start()
    for b in range(BLOCKS):
        load_out(b).start()
    for b in range(BLOCKS):
        load_in(b).start()
    load_head.start()
    load_exon.start()

    @pl.when(p == 0)
    def _():
        for slot in (0, 1):
            trunk[slot, :HALO] = jnp.zeros((HALO, C), jnp.bfloat16)

    @pl.when(p == last)
    def _():
        for slot in (0, 1):
            trunk[slot, HALO + ROWS :] = jnp.zeros((HALO, C), jnp.bfloat16)

    pl.semaphore_wait(barrier, 10 + has_far.astype(jnp.int32))

    def trunk_region(origin, part):
        return trunk.at[0, pl.ds(HALO + part * 192, 192), pl.ds(pl.multiple_of(origin * 384, 128), 384)]

    trunk_ring = Ring(
        trunk_region, z, z_right, z_left, lambda i: trunk_s.at[i], lambda i: trunk_r.at[i],
        own=lambda part: x_ref.at[pl.ds(part * 192, 192)],
    )

    def weights_z(b):
        def region(origin, part):
            return w_out.at[b, origin, core, pl.ds(part * 48, 48), pl.ds(cols_at, 384)]

        def own(part):
            return conv_out_ref.at[b, pl.ds(pl.multiple_of(rows_at + part * 48, 16), 48), pl.ds(cols_at, 384)]

        return Ring(region, z, z_right, z_left, lambda i: wz_s.at[lax.rem(b, 2), i], lambda i: wz_r.at[b, i], own)

    def weights_ring(b):
        def region(origin, part):
            cols = pl.ds(pl.multiple_of(origin * 384, 128), 384)
            return w_out.at[b, pl.ds(part * 2, 2), core, :, cols]

        return Ring(region, ring_me, ring_right, ring_left, lambda i: wr_s.at[lax.rem(b, 2), i], lambda i: wr_r.at[b, i])

    def weights_core(b, half):
        half_b = w_out.at[b, :, half]
        return remote(half_b, half_b, wc_s.at[lax.rem(b, 2)], wc_r.at[b], partner)

    def z_start(b):
        for part in (0, 1):
            weights_z(b).start(part)

    def z_relay(b):
        for part in (0, 1):
            weights_z(b).relay(part)

    def ring_start(b):
        ring = weights_z(b)
        for part in (0, 1):
            ring.gathered(part)
        ring.sent()
        load_out(b).wait()
        for part in (0, 1):
            weights_ring(b).start(part)

    def ring_relay(b):
        for part in (0, 1):
            weights_ring(b).relay(part)

    def core_start(b):
        ring = weights_ring(b)
        for part in (0, 1):
            ring.gathered(part)
        ring.sent()
        weights_core(b, core).start()

    def halo_copies(slot):
        t = trunk.at[slot]
        low = remote(t.at[pl.ds(HALO, HALO)], t.at[pl.ds(HALO + ROWS, HALO)], halo_s.at[slot, 0], halo_r.at[slot, 0], (p - 1, z))
        high = remote(t.at[pl.ds(ROWS, HALO)], t.at[pl.ds(0, HALO)], halo_s.at[slot, 1], halo_r.at[slot, 1], (p + 1, z))
        return low, high

    def halo_start(slot):
        low, high = halo_copies(slot)
        pl.when(p > 0)(low.start)
        pl.when(p < last)(high.start)

    def halo_wait(slot):
        low, high = halo_copies(slot)
        pl.when(p > 0)(high.wait_recv)
        pl.when(p < last)(low.wait_recv)

    def halo_sent(slot):
        low, high = halo_copies(slot)
        pl.when(p > 0)(low.wait_send)
        pl.when(p < last)(high.wait_send)

    def pbias_copy(i, origin, device):
        return remote(pbias_ref, pbias_all.at[origin], pb_s.at[i], pb_r.at[i], device)

    exon_mine = exon_all.at[pl.ds(gene_at, 8)]
    exon_x = exon_all.at[pl.ds(pl.multiple_of(core * 128 + x * 32, 8), 32)]
    exon_core = exon_all.at[pl.ds(pl.multiple_of(core * 128, 8), 128)]

    for part in (0, 1):
        trunk_ring.start(part)
    z_start(0)
    for i in range(3):
        remote(exon_ref, exon_mine, ex_s.at[i], ex_r.at[i], y_peers[i]).start()
        pbias_copy(i, z, z_peers[i]).start()
    for o in range(RING):
        pl.when(z == o)(functools.partial(pbias_all.__setitem__, o, pbias_ref[...]))
    bias_in[:, :HID] = conv_bias_ref[...].astype(jnp.float32)
    for part in (0, 1):
        trunk_ring.relay(part)
    z_relay(0)
    z_start(1)
    load_exon.wait()
    for i in range(3):
        theirs = exon_all.at[pl.ds(pl.multiple_of(core * 128 + x * 32 + lax.rem(y + 3 - i, RING) * 8, 8), 8)]
        remote(theirs, theirs, ex_s.at[i], ex_r.at[i], partner).wait_recv()
    for i in range(3):
        remote(exon_x, exon_x, ex_s.at[3 + i], ex_r.at[3 + i], x_peers[i]).start()
    for part in (0, 1):
        trunk_ring.gathered(part)
    trunk_ring.sent()
    load_x.wait()
    halo_start(0)
    for i in range(3):
        pbias_copy(i, lax.rem(z + 3 - i, RING), partner).wait_recv()
    for o in range(RING):
        bias_out[:, o * 384 : (o + 1) * 384] = pbias_all[o].astype(jnp.float32)
    ring_start(0)
    z_relay(1)
    for i in range(3):
        theirs = exon_all.at[pl.ds(pl.multiple_of(core * 128 + lax.rem(x + 3 - i, RING) * 32, 8), 32)]
        remote(theirs, theirs, ex_s.at[3 + i], ex_r.at[3 + i], partner).wait_recv()
    exon_over = remote(exon_core, exon_core, ex_s.at[6], ex_r.at[6], partner)
    exon_over.start()

    lane = lax.broadcasted_iota(jnp.int32, (G, 128), 1)
    contract_last = (((1,), (1,)), ((), ()))

    def block(b, carry):
        slot = lax.rem(b, 2)
        after = 1 - slot
        now = trunk.at[slot]
        load_in(b).wait()
        taps[1, :ROWS, :HID] = lax.dot_general(
            now[HALO : HALO + ROWS], w_in[b, 1], contract_last, preferred_element_type=jnp.float32
        )
        halo_wait(slot)
        taps[0, :, :HID] = lax.dot_general(
            now[: HALO + ROWS], w_in[b, 0], contract_last, preferred_element_type=jnp.float32
        )
        taps[2, :, :HID] = lax.dot_general(
            now[HALO:], w_in[b, 2], contract_last, preferred_element_type=jnp.float32
        )
        bias = bias_in[pl.ds(b, 1), :]
        for one in range(BLOCKS):

            @pl.when(b == one)
            def _():
                s = BASE_DILATION << one
                for g in range(RING):
                    rows = slice(g * G, (g + 1) * G)
                    early, late = slice(g * G + HALO - s, (g + 1) * G + HALO - s), slice(g * G + s, (g + 1) * G + s)
                    inner[rows, :] = taps[0, early, :] + taps[1, rows, :] + taps[2, late, :]

        def act_region(origin, part):
            return acts.at[slot, origin, part]

        ring = Ring(act_region, z, z_right, z_left, lambda i: act_s.at[slot, i], lambda i: act_r.at[slot, i])
        for chunk, groups in enumerate(GROUPS):
            tails = []
            for i, g in enumerate(groups):
                active = gelu(inner[g * G : (g + 1) * G, :] + bias)
                acts[slot, z, chunk, i * G : (i + 1) * G, :] = active[:, :128].astype(jnp.bfloat16)
                tails.append(active[:, 128:])
            tail = jnp.where(lane < 64, tails[0], pltpu.roll(tails[1], 64, 1))
            acts[slot, z, chunk, 2 * G :, :] = tail.astype(jnp.bfloat16)
            ring.start(chunk)
        halo_sent(slot)

        @pl.when(b == 0)
        def _():
            ring_relay(0)

        for chunk in (0, 1):
            ring.relay(chunk)

        @pl.when(b == 0)
        def _():
            core_start(0)
            remote(exon_core, exon_all.at[pl.ds(pl.multiple_of((1 - core) * 128, 8), 128)], ex_s.at[6], ex_r.at[6], partner).wait_recv()

        @pl.when(b + 1 < BLOCKS)
        def _():
            ring_start(b + 1)

        @pl.when(b < RING)
        def _():
            rows = pl.ds(pl.multiple_of(b * 64, 64), 64)
            wanted = exon_all[rows, :] - p * ROWS
            bins = lax.broadcasted_iota(jnp.int32, (64, ROWS), 1)
            found = jnp.zeros((64, ROWS), jnp.float32)
            for k in range(EXONS):
                found = found + jnp.where(wanted[:, k : k + 1] == bins, 1.0, 0.0)
            onehot[rows, :] = found.astype(jnp.bfloat16)

        for chunk in (0, 1):
            ring.gathered(chunk)
        ring.sent()

        @pl.when(b + 1 < BLOCKS)
        def _():
            ring_relay(b + 1)

        weights_core(b, 1 - core).wait_recv()
        weights_core(b, core).wait_send()

        @pl.when(b + 2 < BLOCKS)
        def _():
            z_start(b + 2)

        for chunk, groups in enumerate(GROUPS):
            heads = [acts[slot, o, chunk, : 2 * G, :] for o in range(RING)]
            ends = [acts[slot, o, chunk, 2 * G :, :].astype(jnp.float32) for o in range(RING)]
            turned = [pltpu.roll(e, 64, 1) for e in ends]
            pair_a = jnp.concatenate(heads[:2], axis=1)
            pair_b = jnp.concatenate(heads[2:], axis=1)
            top = [jnp.where(lane < 64, ends[o], turned[o + 1]) for o in (0, 2)]
            low = [jnp.where(lane < 64, turned[o], ends[o + 1]) for o in (0, 2)]
            rest = jnp.concatenate([jnp.concatenate(top, axis=1), jnp.concatenate(low, axis=1)], axis=0).astype(jnp.bfloat16)

            def column(n, carry):
                cols = pl.ds(pl.multiple_of(n * 256, 256), 256)
                w = [w_out[b, o, :, :, cols].reshape(HID, 256) for o in range(RING)]
                branch = jnp.dot(pair_a, jnp.concatenate([w[0][:128], w[1][:128]], axis=0), preferred_element_type=jnp.float32)
                branch = branch + jnp.dot(pair_b, jnp.concatenate([w[2][:128], w[3][:128]], axis=0), preferred_element_type=jnp.float32)
                branch = branch + jnp.dot(rest, jnp.concatenate([v[128:] for v in w], axis=0), preferred_element_type=jnp.float32)
                add = bias_out[pl.ds(b, 1), cols]
                for i, g in enumerate(groups):
                    rows = pl.ds(HALO + g * G, G)
                    old = trunk[slot, rows, cols].astype(jnp.float32)
                    trunk[after, rows, cols] = (old + branch[i * G : (i + 1) * G] + add).astype(jnp.bfloat16)
                return carry

            lax.fori_loop(0, C // 256, column, 0)
            if chunk == 0:

                @pl.when(b + 1 < BLOCKS)
                def _():
                    halo_start(after)

        @pl.when(b + 1 < BLOCKS)
        def _():
            core_start(b + 1)

        @pl.when(b + 2 < BLOCKS)
        def _():
            z_relay(b + 2)

        return carry

    lax.fori_loop(0, BLOCKS, block, 0)

    load_head.wait()
    mine = pl.ds(pl.multiple_of(core * 128, 128), 128)
    theirs = pl.ds(pl.multiple_of((1 - core) * 128, 128), 128)

    def gene_over(n):
        cols = pl.ds(pl.multiple_of(n * 256, 256), 256)
        return remote(gene_a.at[:, cols], gene_ar.at[:, cols], ga_s.at[n], ga_r.at[n], partner)

    def cov_store(n):
        cols = pl.ds(pl.multiple_of(n * 256, 256), 256)
        return pltpu.make_async_copy(cov.at[:, cols], cov_out.at[:, cols], local.at[15 + n])

    def tracks(n, carry):
        cols = pl.ds(pl.multiple_of(n * 256, 256), 256)
        logits = jnp.dot(trunk[0, HALO : HALO + ROWS], w_head[:, cols], preferred_element_type=jnp.float32)
        covered = softplus(logits + head_bias_ref[:, cols].astype(jnp.float32)).astype(jnp.bfloat16)
        cov[:, cols] = covered
        cov_store(n).start()
        gene_a[:, cols] = jnp.dot(onehot[theirs, :], covered, preferred_element_type=jnp.float32).astype(jnp.bfloat16)
        gene_over(n).start()
        own_sum[:, cols] = jnp.dot(onehot[mine, :], covered, preferred_element_type=jnp.float32)
        return carry

    lax.fori_loop(0, TRACKS // 256, tracks, 0)
    for n in range(TRACKS // 256):
        gene_over(n).wait_recv()
    own_sum[...] = own_sum[...] + gene_ar[...].astype(jnp.float32)
    gene_b[...] = own_sum[...].astype(jnp.bfloat16)

    def gene_x(i):
        rows = pl.ds(pl.multiple_of(lax.rem(x + 1 + i, RING) * 32, 32), 32)
        return remote(gene_b.at[rows], gene_br.at[i], gb_s.at[i], gb_r.at[i], x_peers[i])

    for i in range(3):
        gene_x(i).start()
    for i in range(3):
        gene_x(i).wait_recv()
    total = own_sum[pl.ds(pl.multiple_of(x * 32, 32), 32), :]
    for i in range(3):
        total = total + gene_br[i].astype(jnp.float32)
    gene_c[...] = total

    def gene_y(i):
        rows = pl.ds(pl.multiple_of(lax.rem(y + 1 + i, RING) * 8, 8), 8)
        return remote(gene_c.at[rows], gene_cr.at[i], gc_s.at[i], gc_r.at[i], y_peers[i])

    for i in range(3):
        gene_y(i).start()
    counts = jnp.sum(jnp.where(exon_ref[...] >= 0, 1.0, 0.0), axis=1, keepdims=True)
    for i in range(3):
        gene_y(i).wait_recv()
    total = gene_c[pl.ds(pl.multiple_of(y * 8, 8), 8), :]
    for i in range(3):
        total = total + gene_cr[i]
    gene_out[...] = total / counts

    for i in range(3):
        gene_x(i).wait_send()
        gene_y(i).wait_send()
        remote(exon_ref, exon_mine, ex_s.at[i], ex_r.at[i], partner).wait_send()
        remote(exon_x, exon_x, ex_s.at[3 + i], ex_r.at[3 + i], partner).wait_send()
        pbias_copy(i, z, partner).wait_send()
    exon_over.wait_send()
    for n in range(TRACKS // 256):
        gene_over(n).wait_send()
        cov_store(n).wait()


def shards(trunk_input, conv_in, conv_bias, conv_out, projection_bias, head_weight, head_bias, exon_bins):
    hbm = pl.BlockSpec(memory_space=pl.ANY)
    vmem = pl.BlockSpec(memory_space=pltpu.VMEM)
    bf16, f32 = jnp.bfloat16, jnp.float32
    dma = pltpu.SemaphoreType.DMA
    return pl.pallas_call(
        kernel,
        out_shape=(jax.ShapeDtypeStruct((ROWS, TRACKS), bf16), jax.ShapeDtypeStruct((8, TRACKS), f32)),
        in_specs=[hbm, hbm, vmem, hbm, vmem, hbm, vmem, vmem],
        out_specs=(hbm, vmem),
        scratch_shapes=[
            pltpu.VMEM((2, ROWS + 2 * HALO, C), bf16),
            pltpu.VMEM((BLOCKS, 3, HID, C), bf16),
            pltpu.VMEM((BLOCKS, RING, 2, G, C), bf16),
            pltpu.VMEM((C, TRACKS), bf16),
            pltpu.VMEM((3, ROWS + HALO, 256), f32),
            pltpu.VMEM((ROWS, 256), f32),
            pltpu.VMEM((2, RING, 2, 3 * G, 128), bf16),
            pltpu.VMEM((BLOCKS, 256), f32),
            pltpu.VMEM((BLOCKS, C), f32),
            pltpu.VMEM((RING, BLOCKS, 384), bf16),
            pltpu.VMEM((ROWS, TRACKS), bf16),
            pltpu.VMEM((GENES, EXONS), jnp.int32),
            pltpu.VMEM((GENES, ROWS), bf16),
            pltpu.VMEM((128, TRACKS), f32),
            pltpu.VMEM((128, TRACKS), bf16),
            pltpu.VMEM((128, TRACKS), bf16),
            pltpu.VMEM((128, TRACKS), bf16),
            pltpu.VMEM((3, 32, TRACKS), bf16),
            pltpu.VMEM((32, TRACKS), f32),
            pltpu.VMEM((3, 8, TRACKS), f32),
            dma((19,)),
            dma((6,)), dma((6,)),
            dma((2, 6)), dma((2, 6)),
            dma((2, 6)), dma((BLOCKS, 6)),
            dma((2, 6)), dma((BLOCKS, 6)),
            dma((2,)), dma((BLOCKS,)),
            dma((2, 2)), dma((2, 2)),
            dma((3,)), dma((3,)),
            dma((7,)), dma((7,)),
            dma((4,)), dma((4,)),
            dma((3,)), dma((3,)),
            dma((3,)), dma((3,)),
        ],
        compiler_params=pltpu.CompilerParams(
            collective_id=0, has_side_effects=True, vmem_limit_bytes=60000 * 1024
        ),
        name="trunk",
    )(trunk_input, conv_in, conv_bias, conv_out, projection_bias, head_weight, head_bias.reshape(1, TRACKS), exon_bins)


def solution(mesh):
    in_specs = (
        P("seq", "trk"),
        P(None, None, "trk", None),
        P(None, "trk"),
        P(None, "trk", None),
        P(None, "trk"),
        P(None, "trk"),
        P("trk"),
        P("seq", None),
    )
    out_specs = (P("seq", "trk"), P("seq", "trk"))
    return jax.shard_map(shards, mesh=mesh, in_specs=in_specs, out_specs=out_specs, check_vma=False)
```

```python
import functools

import jax
import jax.numpy as jnp
from jax import lax
from jax.experimental import pallas as pl
from jax.experimental.pallas import tpu as pltpu
from jax.sharding import PartitionSpec as P

MESH = pl.DeviceIdType.MESH
BLOCKS = 6
BASE_DILATION = 2
RING = 4
ROWS = 384
C = 1536
HID = 192
HALO = 64
TRACKS = 1024
GENES = 256
EXONS = 64
G = 96
GROUPS = ((0, 3), (1, 2))


def remote(src, dst, send, recv, device):
    return pltpu.make_async_remote_copy(
        src_ref=src, dst_ref=dst, send_sem=send, recv_sem=recv, device_id=device, device_id_type=MESH
    )


class Ring:
    def __init__(self, region, me, right, left, send, recv, own=None):
        self.region, self.me, self.right, self.left = region, me, right, left
        self.send, self.recv = send, recv
        self.own = own or (lambda part: region(me, part))
        self.before, self.after = lax.rem(me + RING - 1, RING), lax.rem(me + 1, RING)
        self.across = lax.rem(me + 2, RING)

    def copy(self, src, origin, part, way):
        there = self.region(origin, part)
        i = part * 3 + way
        to_right = way == 0 or (way == 2 and part % 2 == 0)
        return remote(src, there, self.send(i), self.recv(i), self.right if to_right else self.left)

    def start(self, pair, turns=(0, 1)):
        for turn in turns:
            for part, way in (((0, 0), (1, 1)), ((1, 0), (0, 1)))[turn]:
                part += 2 * pair
                self.copy(self.own(part), self.me, part, way).start()

    def relay(self, pair):
        for part in (2 * pair, 2 * pair + 1):
            origin = self.before if part % 2 == 0 else self.after
            there = self.region(origin, part)
            self.copy(there, origin, part, part % 2).wait_recv()
            self.copy(there, origin, part, 2).start()

    def gathered(self, pair):
        even, odd = 2 * pair, 2 * pair + 1
        for origin, part, way in ((self.after, even, 1), (self.before, odd, 0), (self.across, even, 2), (self.across, odd, 2)):
            self.copy(self.region(origin, part), origin, part, way).wait_recv()

    def sent(self, pair):
        for part in (2 * pair, 2 * pair + 1):
            for way in (0, 1, 2):
                self.copy(self.own(part) if way < 2 else self.region(self.me, part), self.me, part, way).wait_send()


def gelu(v):
    return v * (0.5 * (1.0 + jnp.tanh(0.7978845608028654 * (v + 0.044715 * (v * v * v)))))


def softplus(logits):
    return jnp.maximum(logits, 0.0) + jnp.log1p(jnp.exp(-jnp.abs(logits)))


def kernel(
    x_ref, conv_in_ref, conv_bias_ref, conv_out_ref, pbias_ref, head_ref, head_bias_ref, exon_ref,
    cov_out, gene_out,
    trunk, w_in, w_out, w_head, taps, inner, acts, bias_in, bias_out, pbias_all, head_bias, cov, exon_all, onehot,
    own_sum, gene_a, gene_ar, gene_b, gene_br, gene_c, gene_cr,
    local, trunk_s, trunk_r, act_s, act_r, wz_s, wz_r, wr_s, wr_r, wc_s, wc_r,
    halo_s, halo_r, pb_s, pb_r, ex_s, ex_r, ga_s, ga_r, gb_s, gb_r, gc_s, gc_r,
):
    p = lax.axis_index("seq")
    z = lax.axis_index("trk")
    core = lax.rem(p, 2)
    y = lax.rem(p // 2, RING)
    x = p // 8
    last = 31

    def at(xx, yy, cc):
        return (lax.rem(xx, RING) * RING + lax.rem(yy, RING)) * 2 + cc

    z_right, z_left = (p, lax.rem(z + 1, RING)), (p, lax.rem(z + 3, RING))
    partner = (p + 1 - 2 * core, z)
    ring_me = x * (1 - core) + y * core
    ring_right = (at(x + 1 - core, y + core, core), z)
    ring_left = (at(x + 3 * (1 - core), y + 3 * core, core), z)
    x_peers = [(at(x + d, y, core), z) for d in (1, 2, 3)]
    y_peers = [(at(x, y + d, core), z) for d in (1, 2, 3)]
    z_peers = [(p, lax.rem(z + d, RING)) for d in (1, 2, 3)]
    barrier = pltpu.get_barrier_semaphore()
    for device in [partner] + x_peers + y_peers + z_peers:
        pl.semaphore_signal(barrier, inc=1, device_id=device, device_id_type=MESH)
    far = p + 2 * core - 1
    has_far = jnp.logical_and(far >= 0, far <= last)

    @pl.when(has_far)
    def _():
        pl.semaphore_signal(barrier, inc=1, device_id=(far, z), device_id_type=MESH)

    def load_in(b):
        return pltpu.make_async_copy(conv_in_ref.at[b], w_in.at[b], local.at[b])

    rows_at, cols_at = pl.multiple_of(core * G, 16), pl.multiple_of(ring_me * 384, 128)

    def load_out(b):
        src = conv_out_ref.at[b, pl.ds(rows_at, G), pl.ds(cols_at, 384)]
        return pltpu.make_async_copy(src, w_out.at[b, z, core, :, pl.ds(cols_at, 384)], local.at[BLOCKS + b])

    z_cols = pl.multiple_of(z * 384, 128)
    load_x = pltpu.make_async_copy(x_ref, trunk.at[0, pl.ds(HALO, ROWS), pl.ds(z_cols, 384)], local.at[12])
    load_head = pltpu.make_async_copy(head_ref, w_head, local.at[13])
    gene_at = pl.multiple_of(core * 128 + x * 32 + y * 8, 8)
    load_exon = pltpu.make_async_copy(exon_ref, exon_all.at[pl.ds(gene_at, 8)], local.at[14])
    load_x.start()
    for b in range(BLOCKS):
        load_out(b).start()
    for b in range(BLOCKS):
        load_in(b).start()
    load_head.start()
    load_exon.start()

    @pl.when(p == 0)
    def _():
        for slot in (0, 1):
            trunk[slot, :HALO] = jnp.zeros((HALO, C), jnp.bfloat16)

    @pl.when(p == last)
    def _():
        for slot in (0, 1):
            trunk[slot, HALO + ROWS :] = jnp.zeros((HALO, C), jnp.bfloat16)

    pl.semaphore_wait(barrier, 10 + has_far.astype(jnp.int32))

    def trunk_region(origin, part):
        return trunk.at[0, pl.ds(HALO + part * 192, 192), pl.ds(pl.multiple_of(origin * 384, 128), 384)]

    trunk_ring = Ring(
        trunk_region, z, z_right, z_left, lambda i: trunk_s.at[i], lambda i: trunk_r.at[i],
        own=lambda part: x_ref.at[pl.ds(part * 192, 192)],
    )

    def weights_z(b):
        def region(origin, part):
            return w_out.at[b, origin, core, pl.ds(part * 48, 48), pl.ds(cols_at, 384)]

        def own(part):
            return conv_out_ref.at[b, pl.ds(pl.multiple_of(rows_at + part * 48, 16), 48), pl.ds(cols_at, 384)]

        return Ring(region, z, z_right, z_left, lambda i: wz_s.at[lax.rem(b, 3), i], lambda i: wz_r.at[b, i], own)

    def weights_ring(b):
        def region(origin, part):
            cols = pl.ds(pl.multiple_of(origin * 384, 128), 384)
            return w_out.at[b, pl.ds(part * 2, 2), core, :, cols]

        return Ring(region, ring_me, ring_right, ring_left, lambda i: wr_s.at[lax.rem(b, 2), i], lambda i: wr_r.at[b, i])

    def weights_core(b, half):
        half_b = w_out.at[b, :, half]
        return remote(half_b, half_b, wc_s.at[lax.rem(b, 2)], wc_r.at[b], partner)

    def ring_start(b):
        weights_z(b).gathered(0)
        weights_z(b).sent(0)
        load_out(b).wait()
        weights_ring(b).start(0)

    def core_start(b):
        weights_ring(b).gathered(0)
        weights_ring(b).sent(0)
        weights_core(b, core).start()

    def halo_copies(slot, rows):
        t = trunk.at[slot]
        low = remote(
            t.at[pl.ds(HALO, rows)], t.at[pl.ds(HALO + ROWS, rows)], halo_s.at[slot, 0], halo_r.at[slot, 0], (p - 1, z)
        )
        high = remote(
            t.at[pl.ds(HALO + ROWS - rows, rows)], t.at[pl.ds(HALO - rows, rows)], halo_s.at[slot, 1], halo_r.at[slot, 1], (p + 1, z)
        )
        return low, high

    def halo_start(slot, rows):
        low, high = halo_copies(slot, rows)
        pl.when(p > 0)(low.start)
        pl.when(p < last)(high.start)

    def halo_wait(slot, rows):
        low, high = halo_copies(slot, rows)
        pl.when(p > 0)(high.wait_recv)
        pl.when(p < last)(low.wait_recv)

    def halo_sent(slot, rows):
        low, high = halo_copies(slot, rows)
        pl.when(p > 0)(low.wait_send)
        pl.when(p < last)(high.wait_send)

    def halo(step, b, slot):
        pl.when(b < 4)(lambda: step(slot, 16))
        for one in (4, 5):
            pl.when(b == one)(lambda: step(slot, BASE_DILATION << one))

    def pbias_copy(i, origin, device):
        return remote(pbias_ref, pbias_all.at[origin], pb_s.at[i], pb_r.at[i], device)

    exon_mine = exon_all.at[pl.ds(gene_at, 8)]
    exon_x = exon_all.at[pl.ds(pl.multiple_of(core * 128 + x * 32, 8), 32)]
    exon_core = exon_all.at[pl.ds(pl.multiple_of(core * 128, 8), 128)]
    weights_z(0).start(0)
    trunk_ring.start(0, (0,))
    for i in range(3):
        remote(exon_ref, exon_mine, ex_s.at[i], ex_r.at[i], y_peers[i]).start()
        pbias_copy(i, z, z_peers[i]).start()
    for o in range(RING):
        pl.when(z == o)(functools.partial(pbias_all.__setitem__, o, pbias_ref[...]))
    bias_in[:, :HID] = conv_bias_ref[...].astype(jnp.float32)
    weights_z(0).relay(0)
    trunk_ring.start(0, (1,))
    trunk_ring.relay(0)
    load_exon.wait()
    for i in range(3):
        theirs = exon_all.at[pl.ds(pl.multiple_of(core * 128 + x * 32 + lax.rem(y + 3 - i, RING) * 8, 8), 8)]
        remote(theirs, theirs, ex_s.at[i], ex_r.at[i], partner).wait_recv()
    for i in range(3):
        remote(exon_x, exon_x, ex_s.at[3 + i], ex_r.at[3 + i], x_peers[i]).start()
    ring_start(0)
    trunk_ring.gathered(0)
    load_x.wait()
    halo_start(0, 16)
    weights_z(1).start(0)
    weights_z(2).start(0)
    trunk_ring.sent(0)
    weights_ring(0).relay(0)
    for i in range(3):
        pbias_copy(i, lax.rem(z + 3 - i, RING), partner).wait_recv()
    for o in range(RING):
        bias_out[:, o * 384 : (o + 1) * 384] = pbias_all[o].astype(jnp.float32)
    for i in range(3):
        theirs = exon_all.at[pl.ds(pl.multiple_of(core * 128 + lax.rem(x + 3 - i, RING) * 32, 8), 32)]
        remote(theirs, theirs, ex_s.at[3 + i], ex_r.at[3 + i], partner).wait_recv()
    exon_over = remote(exon_core, exon_core, ex_s.at[6], ex_r.at[6], partner)
    exon_over.start()
    lane = lax.broadcasted_iota(jnp.int32, (G, 128), 1)
    contract_last = (((1,), (1,)), ((), ()))

    def block(b, carry):
        slot = lax.rem(b, 2)
        after = 1 - slot
        now = trunk.at[slot]
        load_in(b).wait()
        rows = now[HALO : HALO + ROWS]
        for tap, first in ((1, 0), (0, HALO), (2, 0)):
            taps[tap, first : first + ROWS, :HID] = lax.dot_general(
                rows, w_in[b, tap], contract_last, preferred_element_type=jnp.float32
            )
        halo(halo_wait, b, slot)
        taps[0, :HALO, :HID] = lax.dot_general(
            now[:HALO], w_in[b, 0], contract_last, preferred_element_type=jnp.float32
        )
        taps[2, ROWS:, :HID] = lax.dot_general(
            now[HALO + ROWS :], w_in[b, 2], contract_last, preferred_element_type=jnp.float32
        )
        bias = bias_in[pl.ds(b, 1), :]
        for one in range(BLOCKS):

            @pl.when(b == one)
            def _():
                s = BASE_DILATION << one
                for g in range(RING):
                    rows = slice(g * G, (g + 1) * G)
                    early, late = slice(g * G + HALO - s, (g + 1) * G + HALO - s), slice(g * G + s, (g + 1) * G + s)
                    inner[rows, :] = taps[0, early, :] + taps[1, rows, :] + taps[2, late, :]

        def act_region(origin, part):
            return acts.at[slot, origin, part // 2, pl.ds((part % 2) * 144, 144)]

        ring = Ring(act_region, z, z_right, z_left, lambda i: act_s.at[slot, i], lambda i: act_r.at[slot, i])
        for chunk, groups in enumerate(GROUPS):
            tails = []
            for i, g in enumerate(groups):
                active = gelu(inner[g * G : (g + 1) * G, :] + bias)
                acts[slot, z, chunk, i * G : (i + 1) * G, :] = active[:, :128].astype(jnp.bfloat16)
                tails.append(active[:, 128:])
            tail = jnp.where(lane < 64, tails[0], pltpu.roll(tails[1], 64, 1))
            acts[slot, z, chunk, 2 * G :, :] = tail.astype(jnp.bfloat16)
            ring.start(chunk, (0, 1) if chunk == 0 else (0,))
        halo(halo_sent, b, slot)

        @pl.when(b == 0)
        def _():
            core_start(0)

        @pl.when(b == 1)
        def _():
            weights_ring(1).relay(0)

        @pl.when(b > 1)
        def _():
            core_start(b)

        @pl.when(jnp.logical_and(b > 0, b + 1 < BLOCKS))
        def _():
            ring_start(b + 1)
        ring.relay(0)
        ring.start(1, (1,))
        ring.relay(1)
        @pl.when(b == 0)
        def _():
            weights_z(1).relay(0)
            remote(exon_core, exon_all.at[pl.ds(pl.multiple_of((1 - core) * 128, 8), 128)], ex_s.at[6], ex_r.at[6], partner).wait_recv()

        @pl.when(b + 2 < BLOCKS)
        def _():
            weights_z(b + 2).relay(0)

        @pl.when(b == 1)
        def _():
            core_start(1)

        @pl.when(jnp.logical_and(b > 0, b + 1 < BLOCKS))
        def _():
            weights_ring(b + 1).relay(0)
        @pl.when(b < RING)
        def _():
            rows = pl.ds(pl.multiple_of(b * 64, 64), 64)
            wanted = exon_all[rows, :] - p * ROWS
            bins = lax.broadcasted_iota(jnp.int32, (64, ROWS), 1)
            found = jnp.zeros((64, ROWS), jnp.float32)
            for k in range(EXONS):
                found = found + jnp.where(wanted[:, k : k + 1] == bins, 1.0, 0.0)
            onehot[rows, :] = found.astype(jnp.bfloat16)
        weights_core(b, 1 - core).wait_recv()
        weights_core(b, core).wait_send()
        ring.gathered(0)
        for chunk, groups in enumerate(GROUPS):
            heads = [acts[slot, o, chunk, : 2 * G, :] for o in range(RING)]
            ends = [acts[slot, o, chunk, 2 * G :, :].astype(jnp.float32) for o in range(RING)]
            turned = [pltpu.roll(e, 64, 1) for e in ends]
            top = [jnp.where(lane < 64, ends[o], turned[o + 1]) for o in (0, 2)]
            low = [jnp.where(lane < 64, turned[o], ends[o + 1]) for o in (0, 2)]
            rest = jnp.concatenate([jnp.concatenate(top, axis=1), jnp.concatenate(low, axis=1)], axis=0).astype(jnp.bfloat16)
            hidden = jnp.concatenate(heads + [rest], axis=1)

            def column(n, carry):
                cols = pl.ds(pl.multiple_of(n * 256, 256), 256)
                w = [w_out[b, o, :, :, cols].reshape(HID, 256) for o in range(RING)]
                w = jnp.concatenate([v[:128] for v in w] + [v[128:] for v in w], axis=0)
                branch = jnp.dot(hidden, w, preferred_element_type=jnp.float32)
                add = bias_out[pl.ds(b, 1), cols]
                for i, g in enumerate(groups):
                    rows = pl.ds(HALO + g * G, G)
                    old = trunk[slot, rows, cols].astype(jnp.float32)
                    trunk[after, rows, cols] = (old + branch[i * G : (i + 1) * G] + add).astype(jnp.bfloat16)
                return carry

            lax.fori_loop(0, C // 256, column, 0, unroll=True)
            if chunk == 0:
                @pl.when(b + 1 < BLOCKS)
                def _():
                    halo(halo_start, b + 1, after)
                ring.gathered(1)
                for pair in (0, 1):
                    ring.sent(pair)

                @pl.when(b + 3 < BLOCKS)
                def _():
                    weights_z(b + 3).start(0)

                @pl.when(b == 0)
                def _():
                    ring_start(1)
        return carry

    lax.fori_loop(0, BLOCKS, block, 0)

    head_bias[...] = head_bias_ref[...].astype(jnp.float32).reshape(1, TRACKS)
    load_head.wait()
    mine = pl.ds(pl.multiple_of(core * 128, 128), 128)
    theirs = pl.ds(pl.multiple_of((1 - core) * 128, 128), 128)

    def columns(n):
        return slice(n * 256, (n + 1) * 256)

    def gene_over(n):
        cols = columns(n)
        return remote(gene_a.at[:, cols], gene_ar.at[:, cols], ga_s.at[n], ga_r.at[n], partner)

    def gene_x(n, i):
        rows = pl.ds(pl.multiple_of(lax.rem(x + 1 + i, RING) * 32, 32), 32)
        cols = columns(n)
        return remote(gene_b.at[rows, cols], gene_br.at[i, :, cols], gb_s.at[n, i], gb_r.at[n, i], x_peers[i])

    def gene_y(n, i):
        rows = pl.ds(pl.multiple_of(lax.rem(y + 1 + i, RING) * 8, 8), 8)
        cols = columns(n)
        return remote(gene_c.at[rows, cols], gene_cr.at[i, :, cols], gc_s.at[n, i], gc_r.at[n, i], y_peers[i])

    def cov_store(n):
        return pltpu.make_async_copy(cov.at[:, columns(n)], cov_out.at[:, columns(n)], local.at[15 + n])

    def both_cores(n):
        cols = columns(n)
        gene_over(n).wait_recv()
        total = own_sum[:, cols] + gene_ar[:, cols].astype(jnp.float32)
        own_sum[:, cols] = total
        gene_b[:, cols] = total.astype(jnp.bfloat16)
        for i in range(3):
            gene_x(n, i).start()

    parts = TRACKS // 256
    for n in range(parts):
        cols = columns(n)
        logits = jnp.dot(trunk[0, HALO : HALO + ROWS], w_head[:, cols], preferred_element_type=jnp.float32)
        covered = softplus(logits + head_bias[:, cols]).astype(jnp.bfloat16)
        cov[:, cols] = covered
        cov_store(n).start()
        gene_a[:, cols] = jnp.dot(onehot[theirs, :], covered, preferred_element_type=jnp.float32).astype(jnp.bfloat16)
        gene_over(n).start()
        own_sum[:, cols] = jnp.dot(onehot[mine, :], covered, preferred_element_type=jnp.float32)
        if n > 0:
            both_cores(n - 1)
    both_cores(parts - 1)
    counts = jnp.sum(jnp.where(exon_ref[...] >= 0, 1.0, 0.0), axis=1, keepdims=True)
    for n in range(parts):
        cols = columns(n)
        total = own_sum[pl.ds(pl.multiple_of(x * 32, 32), 32), cols]
        for i in range(3):
            gene_x(n, i).wait_recv()
            total = total + gene_br[i, :, cols].astype(jnp.float32)
        gene_c[:, cols] = total
        for i in range(3):
            gene_y(n, i).start()
    for n in range(parts):
        cols = columns(n)
        total = gene_c[pl.ds(pl.multiple_of(y * 8, 8), 8), cols]
        for i in range(3):
            gene_y(n, i).wait_recv()
            total = total + gene_cr[i, :, cols]
        gene_out[:, cols] = total / counts
    for i in range(3):
        for n in range(parts):
            gene_x(n, i).wait_send()
            gene_y(n, i).wait_send()
        remote(exon_ref, exon_mine, ex_s.at[i], ex_r.at[i], partner).wait_send()
        remote(exon_x, exon_x, ex_s.at[3 + i], ex_r.at[3 + i], partner).wait_send()
        pbias_copy(i, z, partner).wait_send()
    exon_over.wait_send()
    for n in range(parts):
        gene_over(n).wait_send()
        cov_store(n).wait()


def shards(trunk_input, conv_in, conv_bias, conv_out, projection_bias, head_weight, head_bias, exon_bins):
    hbm = pl.BlockSpec(memory_space=pl.ANY)
    vmem = pl.BlockSpec(memory_space=pltpu.VMEM)
    bf16, f32 = jnp.bfloat16, jnp.float32
    dma = pltpu.SemaphoreType.DMA
    return pl.pallas_call(
        kernel,
        out_shape=(jax.ShapeDtypeStruct((ROWS, TRACKS), bf16), jax.ShapeDtypeStruct((8, TRACKS), f32)),
        in_specs=[hbm, hbm, vmem, hbm, vmem, hbm, vmem, vmem],
        out_specs=(hbm, vmem),
        scratch_shapes=[
            pltpu.VMEM((2, ROWS + 2 * HALO, C), bf16),
            pltpu.VMEM((BLOCKS, 3, HID, C), bf16),
            pltpu.VMEM((BLOCKS, RING, 2, G, C), bf16),
            pltpu.VMEM((C, TRACKS), bf16),
            pltpu.VMEM((3, ROWS + HALO, 256), f32),
            pltpu.VMEM((ROWS, 256), f32),
            pltpu.VMEM((2, RING, 2, 3 * G, 128), bf16),
            pltpu.VMEM((BLOCKS, 256), f32),
            pltpu.VMEM((BLOCKS, C), f32),
            pltpu.VMEM((RING, BLOCKS, 384), bf16),
            pltpu.VMEM((1, TRACKS), f32),
            pltpu.VMEM((ROWS, TRACKS), bf16),
            pltpu.VMEM((GENES, EXONS), jnp.int32),
            pltpu.VMEM((GENES, ROWS), bf16),
            pltpu.VMEM((128, TRACKS), f32),
            pltpu.VMEM((128, TRACKS), bf16),
            pltpu.VMEM((128, TRACKS), bf16),
            pltpu.VMEM((128, TRACKS), bf16),
            pltpu.VMEM((3, 32, TRACKS), bf16),
            pltpu.VMEM((32, TRACKS), f32),
            pltpu.VMEM((3, 8, TRACKS), f32),
            dma((19,)),
            dma((6,)), dma((6,)),
            dma((2, 12)), dma((2, 12)),
            dma((3, 6)), dma((BLOCKS, 6)),
            dma((2, 6)), dma((BLOCKS, 6)),
            dma((2,)), dma((BLOCKS,)),
            dma((2, 2)), dma((2, 2)),
            dma((3,)), dma((3,)),
            dma((7,)), dma((7,)),
            dma((4,)), dma((4,)),
            dma((4, 3)), dma((4, 3)),
            dma((4, 3)), dma((4, 3)),
        ],
        compiler_params=pltpu.CompilerParams(
            collective_id=0, has_side_effects=True, vmem_limit_bytes=60000 * 1024
        ),
        name="trunk",
    )(trunk_input, conv_in, conv_bias, conv_out, projection_bias, head_weight, head_bias, exon_bins)


def solution(mesh):
    in_specs = (
        P("seq", "trk"),
        P(None, None, "trk", None),
        P(None, "trk"),
        P(None, "trk", None),
        P(None, "trk"),
        P(None, "trk"),
        P("trk"),
        P("seq", None),
    )
    out_specs = (P("seq", "trk"), P("seq", "trk"))
    return jax.shard_map(shards, mesh=mesh, in_specs=in_specs, out_specs=out_specs, check_vma=False)
```
